32 devices in a mesh: owner: 8 (over z, core), helper: 4 (over y, x).
Axes of the slice: x: 2, y: 2, z: 4, core: 2. Of those that a mesh axis runs over, the one named last changes fastest.
Arguments:
- points: bfloat16 [128, 64, 512], P(('owner', 'helper')), may hold values from -1.5 to 1.5
- weights: bfloat16 [128, 16, 512], P(('owner', 'helper')), may hold values from -6 to 6
- neighbours: int32 [128, 32], P(('owner', 'helper')), may hold values from -1 to 127, as said below
- counts: int32 [128], P(('owner', 'helper')), may hold values from 1 to 32, as said below
Outputs:
- potential: float32 [128, 16, 512], P(('owner', 'helper'))
The draws below stay inside these ranges and needn't reach their ends.
Inputs may be any that keep to these rules, and one draw needn't show every extreme that they name: `neighbours`: slot 0 of a leaf's list holds the leaf itself; slots 0 to counts - 1 hold distinct leaves, each in the same group of 16 consecutive leaves as the listed leaf or in the group just before or just after it; all other slots hold -1. `counts`: some leaf has a full list in every draw.
All inputs are finite; a program needn't handle non-finite values.
Results may differ from the reference program's by a relative error of at most 0.0028.
Values may be sent and summed in bfloat16 or wider, within the bound.
A program may use at most 64 MiB of HBM per device.

```python
import jax
import jax.numpy as jnp
from jax import lax

DIM = 64
NV = 16
LEAF = 512
GROUP = 16
LEAVES = 128
MAXNB = 32


def make_lists(key):
    base_key = jax.random.fold_in(key, 31)
    heavy_key, forced_key, light_key, score_key = jax.random.split(base_key, 4)
    leaf_ids = jnp.arange(LEAVES, dtype=jnp.int32)
    heavy = jax.random.randint(heavy_key, (LEAVES,), 0, 8) == 0
    forced = jax.random.randint(forced_key, (), 0, LEAVES)
    heavy = heavy | (leaf_ids == forced)
    light = jax.random.randint(light_key, (LEAVES,), 1, MAXNB // 4 + 1)
    sizes = jnp.where(heavy, MAXNB, light).astype(jnp.int32)
    offsets = jnp.arange(3 * GROUP, dtype=jnp.int32)
    starts = (leaf_ids // GROUP - 1) * GROUP
    candidates = starts[:, None] + offsets[None, :]
    usable = (candidates >= 0) & (candidates < LEAVES) & (candidates != leaf_ids[:, None])
    scores = jax.random.randint(score_key, (LEAVES, 3 * GROUP), 0, 1 << 20) * (3 * GROUP) + offsets[None, :]
    scores = jnp.where(usable, scores, -1)
    picked_scores, picked = lax.top_k(scores, MAXNB - 1)
    chosen = jnp.take_along_axis(candidates, picked, axis=1)
    lists = jnp.concatenate([leaf_ids[:, None], chosen], axis=1)
    slots = jnp.arange(MAXNB, dtype=jnp.int32)
    lists = jnp.where(slots[None, :] < sizes[:, None], lists, -1)
    return (lists.astype(jnp.int32), sizes)


def draw_neighbours(key, part):
    lists, sizes = make_lists(key)
    return lists


def draw_counts(key, part):
    lists, sizes = make_lists(key)
    return sizes


def block_scale(rng, dims, cuts, smallest, high):
    def one(dim, shards_of):
        heights = jax.random.uniform(jax.random.fold_in(jax.random.fold_in(rng, 6), dim), (shards_of,), jnp.float32, smallest / len(cuts), high / len(cuts))
        return jnp.repeat(jnp.exp(heights), dims[dim] // shards_of).reshape((-1,) + (1,) * (len(dims) - dim - 1))

    factor_of = one(*cuts[0])
    for cut in cuts[1:]:
        factor_of = factor_of * one(*cut)
    return factor_of


def noise(key, shape, spread, reach, shards=(), held_as=jnp.bfloat16):
    entries = jax.random.normal(key, shape, jnp.float32) * spread
    if len(shards) > 0:
        entries = block_scale(key, shape, shards, -0.22, 0.18) * entries
    return jnp.clip(entries, min=-reach, max=reach).astype(held_as)


def setup_inputs(seed: int = 0) -> dict:
    key_of = jax.random.split(jax.random.key(seed), 5)
    return {
        "points": noise(key_of[0], (LEAVES, DIM, LEAF), (2.0 / DIM ** 0.5), 1.5, ((0, 32),)),
        "weights": noise(key_of[1], (LEAVES, NV, LEAF), 1.0, 6.0, ((0, 32),)),
        "neighbours": draw_neighbours(jax.random.fold_in(key_of[4], 71), 0),
        "counts": draw_counts(jax.random.fold_in(key_of[4], 71), 0),
    }


def block_sum(target_points, target_norms, source_points, source_norms, source_weights):
    inner = lax.dot_general(source_points, target_points, (((0,), (0,)), ((), ())), preferred_element_type=jnp.float32)
    kernel = jnp.exp(inner - 0.5 * source_norms[:, None] - 0.5 * target_norms[None, :]).astype(jnp.bfloat16)
    return jnp.dot(source_weights, kernel, preferred_element_type=jnp.float32)


def reference(points, weights, neighbours, counts):
    widened = points.astype(jnp.float32)
    norms = jnp.einsum("ldp,ldp->lp", widened, widened)

    def one_leaf(leaf):
        def add_pair(slot, total):
            source = neighbours[leaf, slot]
            return total + block_sum(points[leaf], norms[leaf], points[source], norms[source], weights[source])

        start = jnp.zeros((weights.shape[1], points.shape[2]), jnp.float32)
        return lax.fori_loop(0, counts[leaf], add_pair, start)

    return lax.map(one_leaf, jnp.arange(points.shape[0], dtype=jnp.int32))
```

```python
import functools
import math

import jax
import jax.numpy as jnp
from jax import lax
from jax.experimental import pallas as pl
from jax.experimental.pallas import tpu as pltpu
from jax.sharding import PartitionSpec as P

MESH = pl.DeviceIdType.MESH
LOG2E = math.log2(math.e)
PIECES = 3
DEPTH = 256


def partner_of(index, distance):
    result = index
    bit = 1
    while bit <= distance:
        if distance & bit:
            result = result + bit - 2 * bit * ((index // bit) % 2)
        bit *= 2
    return result


def gather_kernel(owners, helpers, points, weights, lists, far_points, near_points, near_weights, far_lists,
                  send_sems, recv_sems):
    owner = lax.axis_index("owner")
    helper = lax.axis_index("helper")
    has_before = owner > 0
    has_after = owner < owners - 1
    barrier = pltpu.get_barrier_semaphore()
    for distance in range(1, helpers):
        pl.semaphore_signal(
            barrier, inc=1, device_id=(owner, partner_of(helper, distance)), device_id_type=MESH
        )

    @pl.when(has_before)
    def _():
        pl.semaphore_signal(barrier, inc=1, device_id=(owner - 1, helper), device_id_type=MESH)

    @pl.when(has_after)
    def _():
        pl.semaphore_signal(barrier, inc=1, device_id=(owner + 1, helper), device_id_type=MESH)

    neighbours = lax.min(owner, 1) + lax.min(owners - 1 - owner, 1)
    pl.semaphore_wait(barrier, helpers - 1 + neighbours)

    def copy(number, src, dst, device):
        return pltpu.make_async_remote_copy(
            src_ref=src,
            dst_ref=dst,
            send_sem=send_sems.at[number],
            recv_sem=recv_sems.at[number],
            device_id=device,
            device_id_type=MESH,
        )

    inner = []
    for distance in range(1, helpers):
        device = (owner, partner_of(helper, distance))
        inner.append(copy(len(inner), points, far_points.at[distance - 1], device))
        inner.append(copy(len(inner), lists, far_lists.at[distance - 1], device))
    first = len(inner)
    up = [
        copy(first, points, near_points.at[0], (owner + 1, helper)),
        copy(first + 1, weights, near_weights.at[0], (owner + 1, helper)),
    ]
    down = [
        copy(first + 2, points, near_points.at[1], (owner - 1, helper)),
        copy(first + 3, weights, near_weights.at[1], (owner - 1, helper)),
    ]
    for one in inner:
        one.start()

    @pl.when(has_after)
    def _():
        for one in up:
            one.start()

    @pl.when(has_before)
    def _():
        for one in down:
            one.start()

    for one in inner:
        one.wait()

    @pl.when(has_after)
    def _():
        for one in up:
            one.wait_send()
        for one in down:
            one.wait_recv()

    @pl.when(has_before)
    def _():
        for one in down:
            one.wait_send()
        for one in up:
            one.wait_recv()


def gather_window(owners, helpers, points, weights, lists):
    copies = 2 * (helpers - 1) + 4
    any_space = pl.BlockSpec(memory_space=pl.ANY)
    return pl.pallas_call(
        functools.partial(gather_kernel, owners, helpers),
        out_shape=(
            jax.ShapeDtypeStruct((helpers - 1,) + points.shape, points.dtype),
            jax.ShapeDtypeStruct((2,) + points.shape, points.dtype),
            jax.ShapeDtypeStruct((2,) + weights.shape, weights.dtype),
            jax.ShapeDtypeStruct((helpers - 1,) + lists.shape, lists.dtype),
        ),
        in_specs=[any_space] * 3,
        out_specs=(any_space,) * 4,
        scratch_shapes=[pltpu.SemaphoreType.DMA((copies,)), pltpu.SemaphoreType.DMA((copies,))],
        compiler_params=pltpu.CompilerParams(collective_id=0, has_side_effects=True),
        name="gather_window",
    )(points, weights, lists)


def pieces_of(value, count):
    parts = []
    for _ in range(count):
        part = value.astype(jnp.bfloat16).astype(jnp.float32)
        parts.append(part)
        value = value - part
    return parts


def extra_rows(first, second, rows, width):
    row = lax.broadcasted_iota(jnp.int32, (rows, width), 0)
    result = jnp.zeros((rows, width), jnp.float32)
    for i, value in enumerate(list(first) + list(second)):
        result = jnp.where(row == i, value, result)
    return result


def pairs_kernel(local, helpers, slots, own_lists, far_lists, points, weights, far_points, near_points, near_weights,
                 out, targets, sources, held_weights, tasks):
    owner = lax.axis_index("owner")
    helper = lax.axis_index("helper")
    dims, width = points.shape[1:]
    group = local * helpers
    base = (owner - 1) * group
    extra = DEPTH - PIECES * dims
    ones = [jnp.ones((1, width), jnp.float32)] * 3

    def half_norm(value):
        return pieces_of((-0.5 * LOG2E) * jnp.sum(value * value, axis=0, keepdims=True), 3)

    def prepare_target(index, block):
        value = block.astype(jnp.float32)
        for piece in range(PIECES):
            targets[index, pl.ds(piece * dims, dims), :] = block
        targets[index, pl.ds(PIECES * dims, extra), :] = extra_rows(
            ones, half_norm(value), extra, width
        ).astype(jnp.bfloat16)

    def prepare_source(index, block):
        value = block.astype(jnp.float32)
        rows = pieces_of(value * LOG2E, PIECES) + [extra_rows(half_norm(value), ones, extra, width)]
        sources[index] = jnp.concatenate(rows, axis=0).T.astype(jnp.bfloat16)

    def each_leaf(leaf, carry):
        prepare_target(leaf, points[leaf])
        prepare_source(local + leaf, points[leaf])
        prepare_source(leaf, near_points[0, leaf])
        prepare_source(2 * local + leaf, near_points[1, leaf])
        held_weights[leaf] = near_weights[0, leaf]
        held_weights[local + leaf] = weights[leaf]
        held_weights[2 * local + leaf] = near_weights[1, leaf]
        return carry

    lax.fori_loop(0, local, each_leaf, 0)

    def each_far(number, carry):
        prepare_target(local + number, far_points[number // local, number % local])
        return carry

    lax.fori_loop(0, (helpers - 1) * local, each_far, 0)

    def collect(read, target, count):
        def more(state):
            slot, _ = state
            return (slot < slots) & (read(lax.min(slot, slots - 1)) >= 0)

        def step(state):
            slot, count = state
            place = read(slot) - base
            inside = lax.rem(place, group)
            mine = lax.div(inside, local) == helper
            source = lax.div(place, group) * local + lax.rem(inside, local)
            tasks[count] = target * (3 * local) + source
            return slot + 1, count + mine.astype(jnp.int32)

        return lax.while_loop(more, step, (jnp.int32(0), count))[1]

    def collect_own(leaf, count):
        return collect(lambda slot: own_lists[leaf, slot], leaf, count)

    def collect_far(number, count):
        return collect(
            lambda slot: far_lists[lax.div(number, local), lax.rem(number, local), slot], local + number, count
        )

    total = lax.fori_loop(0, local, collect_own, jnp.int32(0))
    total = lax.fori_loop(0, (helpers - 1) * local, collect_far, total)
    out[...] = jnp.zeros(out.shape, jnp.float32)

    def each_task(number, carry):
        task = tasks[number]
        target = lax.div(task, 3 * local)
        source = lax.rem(task, 3 * local)
        exponent = jnp.dot(sources[source], targets[target], preferred_element_type=jnp.float32)
        kernel = jnp.exp2(exponent).astype(jnp.bfloat16)
        out[target] += jnp.dot(held_weights[source], kernel, preferred_element_type=jnp.float32)
        return carry

    lax.fori_loop(0, total, each_task, 0)


def sum_pairs(helpers, points, weights, lists, far_points, near_points, near_weights, far_lists):
    local, dims, width = points.shape
    vectors = weights.shape[1]
    slots = lists.shape[1]
    group = local * helpers
    vmem = pl.BlockSpec(memory_space=pltpu.VMEM)
    smem = pl.BlockSpec(memory_space=pltpu.SMEM)
    return pl.pallas_call(
        functools.partial(pairs_kernel, local, helpers, slots),
        out_shape=jax.ShapeDtypeStruct((group, vectors, width), jnp.float32),
        in_specs=[smem, smem] + [vmem] * 5,
        out_specs=vmem,
        scratch_shapes=[
            pltpu.VMEM((group, DEPTH, width), jnp.bfloat16),
            pltpu.VMEM((3 * local, width, DEPTH), jnp.bfloat16),
            pltpu.VMEM((3 * local, vectors, width), jnp.bfloat16),
            pltpu.SMEM((group * 3 * local + 1,), jnp.int32),
        ],
        name="sum_pairs",
    )(lists, far_lists, points, weights, far_points, near_points, near_weights)


def return_kernel(helpers, partial, out, landed, send_sems, recv_sems):
    owner = lax.axis_index("owner")
    helper = lax.axis_index("helper")
    barrier = pltpu.get_barrier_semaphore()
    for distance in range(1, helpers):
        pl.semaphore_signal(
            barrier, inc=1, device_id=(owner, partner_of(helper, distance)), device_id_type=MESH
        )
    pl.semaphore_wait(barrier, helpers - 1)
    copies = []
    for distance in range(1, helpers):
        one = pltpu.make_async_remote_copy(
            src_ref=partial.at[distance],
            dst_ref=landed.at[distance - 1],
            send_sem=send_sems.at[distance - 1],
            recv_sem=recv_sems.at[distance - 1],
            device_id=(owner, partner_of(helper, distance)),
            device_id_type=MESH,
        )
        one.start()
        copies.append(one)
    total = partial[0]
    for distance, one in enumerate(copies):
        one.wait_recv()
        total = total + landed[distance]
    out[...] = total
    for one in copies:
        one.wait_send()


def return_sums(helpers, partial):
    shape = partial.shape[1:]
    vmem = pl.BlockSpec(memory_space=pltpu.VMEM)
    return pl.pallas_call(
        functools.partial(return_kernel, helpers),
        out_shape=jax.ShapeDtypeStruct(shape, jnp.float32),
        in_specs=[vmem],
        out_specs=vmem,
        scratch_shapes=[
            pltpu.VMEM((helpers - 1,) + shape, jnp.float32),
            pltpu.SemaphoreType.DMA((helpers - 1,)),
            pltpu.SemaphoreType.DMA((helpers - 1,)),
        ],
        compiler_params=pltpu.CompilerParams(collective_id=1, has_side_effects=True),
        name="return_sums",
    )(partial)


def on_device(points, weights, neighbours, counts):
    local = points.shape[0]
    owners = lax.axis_size("owner")
    helpers = lax.axis_size("helper")
    far_points, near_points, near_weights, far_lists = gather_window(owners, helpers, points, weights, neighbours)
    sums = sum_pairs(helpers, points, weights, neighbours, far_points, near_points, near_weights, far_lists)
    return return_sums(helpers, sums.reshape((helpers, local) + sums.shape[1:]))


def solution(mesh):
    placed = (
        P(("owner", "helper"), None, None),
        P(("owner", "helper"), None, None),
        P(("owner", "helper"), None),
        P(("owner", "helper")),
    )
    return jax.shard_map(
        on_device,
        mesh=mesh,
        in_specs=placed,
        out_specs=P(("owner", "helper"), None, None),
        check_vma=False,
    )
```

```python
import functools

import jax
import jax.numpy as jnp
from jax import lax
from jax.experimental import pallas as pl
from jax.experimental.pallas import tpu as pltpu
from jax.sharding import PartitionSpec as P

MESH = pl.DeviceIdType.MESH
EXTRA = 16
TOGETHER = 4


def partner_of(index, distance):
    result = index
    bit = 1
    while bit <= distance:
        if distance & bit:
            result = result + bit - 2 * bit * ((index // bit) % 2)
        bit *= 2
    return result


def list_tasks(base, helper, local, lists):
    group, slots = lists.shape
    count = 3 * local
    length = task_length(group, local)
    lists = jnp.where(lists < 0, -(1 << 20), lists)
    column = lax.broadcasted_iota(jnp.int32, (group, 128), 1)
    listed = []
    table = jnp.zeros((group, 128), jnp.float32)
    for source in range(count):
        leaf = base + (source // local) * group + helper * local + source % local
        one = jnp.max(jnp.where(lists == leaf, 1.0, 0.0), axis=1, keepdims=True)
        listed.append(one)
        table = jnp.where(column == source, one, table)
    below = lax.broadcasted_iota(jnp.int32, (group, group), 0) > lax.broadcasted_iota(jnp.int32, (group, group), 1)
    ahead = jnp.dot(
        jnp.where(below, 1.0, 0.0).astype(jnp.bfloat16), table.astype(jnp.bfloat16), preferred_element_type=jnp.float32
    )
    place = lax.broadcasted_iota(jnp.int32, (group, length), 1).astype(jnp.float32)
    row = lax.broadcasted_iota(jnp.int32, (group, length), 0).astype(jnp.float32)
    total = jnp.zeros((1, 1), jnp.float32)
    targets = jnp.zeros((group, length), jnp.float32)
    sources = jnp.zeros((group, length), jnp.float32)
    for source in range(count):
        here = jnp.where(listed[source] > 0.5, ahead[:, source:source + 1] + total, -1.0)
        targets = jnp.where(place == here, row, targets)
        sources = jnp.where(place == here, float(source), sources)
        total = total + jnp.sum(listed[source], axis=0, keepdims=True)
    target = jnp.where(place[:1] < total, jnp.sum(targets, axis=0, keepdims=True), float(group))
    source = jnp.sum(sources, axis=0, keepdims=True)
    line = lax.broadcasted_iota(jnp.int32, (8, length), 0)
    result = jnp.where(line == 0, target, jnp.where(line == 1, source, total))
    return result.astype(jnp.int32)


def task_length(group, local):
    return -(-(group * 3 * local + 3 * TOGETHER) // 128) * 128


def gather_kernel(owners, helpers, points, weights, lists, far_points, near_points, near_weights, tasks,
                  far_lists, send_sems, recv_sems):
    local = lists.shape[0]
    owner = lax.axis_index("owner")
    helper = lax.axis_index("helper")
    has_before = owner > 0
    has_after = owner < owners - 1
    barrier = pltpu.get_barrier_semaphore()
    for distance in range(1, helpers):
        pl.semaphore_signal(
            barrier, inc=1, device_id=(owner, partner_of(helper, distance)), device_id_type=MESH
        )

    @pl.when(has_before)
    def _():
        pl.semaphore_signal(barrier, inc=1, device_id=(owner - 1, helper), device_id_type=MESH)

    @pl.when(has_after)
    def _():
        pl.semaphore_signal(barrier, inc=1, device_id=(owner + 1, helper), device_id_type=MESH)

    neighbours = lax.min(owner, 1) + lax.min(owners - 1 - owner, 1)
    pl.semaphore_wait(barrier, helpers - 1 + neighbours)

    def copy(number, src, dst, device):
        return pltpu.make_async_remote_copy(
            src_ref=src,
            dst_ref=dst,
            send_sem=send_sems.at[number],
            recv_sem=recv_sems.at[number],
            device_id=device,
            device_id_type=MESH,
        )

    def beside(distance):
        return (owner, partner_of(helper, distance))

    number = 0
    list_copies = []
    for distance in range(1, helpers):
        list_copies.append(copy(number, lists, far_lists.at[distance - 1], beside(distance)))
        number += 1
    sent, relayed = [], []
    if helpers == 4 and local % 2 == 0:
        half = local // 2
        parts = (pl.ds(0, half), pl.ds(half, half))
        for order in (0, 1):
            for distance in (1, 2):
                part = parts[order if distance == 1 else 1 - order]
                one = copy(number, points.at[part], far_points.at[distance - 1, part], beside(distance))
                number += 1
                sent.append(one)
        for distance in (1, 2):
            part = parts[distance - 1]
            block = far_points.at[distance - 1, part]
            one = copy(number, block, far_points.at[2, part], beside(3 - distance))
            number += 1
            relayed.append(one)
    else:
        for distance in range(1, helpers):
            sent.append(copy(number, points, far_points.at[distance - 1], beside(distance)))
            number += 1
    up = [
        copy(number, points, near_points.at[0], (owner + 1, helper)),
        copy(number + 1, weights, near_weights.at[0], (owner + 1, helper)),
    ]
    down = [
        copy(number + 2, points, near_points.at[1], (owner - 1, helper)),
        copy(number + 3, weights, near_weights.at[1], (owner - 1, helper)),
    ]
    for one in list_copies + sent:
        one.start()

    @pl.when(has_after)
    def _():
        for one in up:
            one.start()

    @pl.when(has_before)
    def _():
        for one in down:
            one.start()

    for place, one in enumerate(relayed):
        sent[place].wait_recv()
        one.start()
    for one in list_copies:
        one.wait_recv()
    whole = jnp.concatenate([lists[...]] + [far_lists[i] for i in range(helpers - 1)], axis=0)
    tasks[...] = list_tasks((owner - 1) * local * helpers, helper, local, whole)
    for one in sent[len(relayed):] + relayed:
        one.wait_recv()
    for one in list_copies + sent + relayed:
        one.wait_send()

    @pl.when(has_after)
    def _():
        for one in up:
            one.wait_send()
        for one in down:
            one.wait_recv()

    @pl.when(has_before)
    def _():
        for one in down:
            one.wait_send()
        for one in up:
            one.wait_recv()


def gather_window(owners, helpers, points, weights, lists):
    local = points.shape[0]
    copies = 2 * (helpers - 1) + 10
    vmem = pl.BlockSpec(memory_space=pltpu.VMEM)
    any_space = pl.BlockSpec(memory_space=pl.ANY)
    return pl.pallas_call(
        functools.partial(gather_kernel, owners, helpers),
        out_shape=(
            jax.ShapeDtypeStruct((helpers - 1,) + points.shape, points.dtype),
            jax.ShapeDtypeStruct((2,) + points.shape, points.dtype),
            jax.ShapeDtypeStruct((2,) + weights.shape, weights.dtype),
            jax.ShapeDtypeStruct((8, task_length(local * helpers, local)), jnp.int32),
        ),
        in_specs=[any_space, any_space, vmem],
        out_specs=(any_space, any_space, any_space, vmem),
        scratch_shapes=[
            pltpu.VMEM((helpers - 1,) + lists.shape, lists.dtype),
            pltpu.SemaphoreType.DMA((copies,)),
            pltpu.SemaphoreType.DMA((copies,)),
        ],
        compiler_params=pltpu.CompilerParams(collective_id=0, has_side_effects=True),
        name="gather_window",
    )(points, weights, lists)


def pieces_of(value, count):
    parts = []
    for _ in range(count):
        part = value.astype(jnp.bfloat16).astype(jnp.float32)
        parts.append(part)
        value = value - part
    return parts


def extra_rows(first, second, rows, width):
    row = lax.broadcasted_iota(jnp.int32, (rows, width), 0)
    result = jnp.zeros((rows, width), jnp.float32)
    for i, value in enumerate(list(first) + list(second)):
        result = jnp.where(row == i, value, result)
    return result


def pairs_kernel(local, helpers, tasks, points, weights, far_points, near_points, near_weights,
                 own_sums, far_sums, out, targets, sources, held_weights, exponents, kernels):
    dims, width = points.shape[1:]
    group = local * helpers
    depth = targets.shape[1]
    ones = [jnp.ones((1, width), jnp.float32)] * 3

    def half_norm(value):
        return pieces_of(-0.5 * jnp.sum(value * value, axis=0, keepdims=True), 3)

    def prepare_target(index, block):
        targets[index, pl.ds(0, dims), :] = block
        targets[index, pl.ds(dims, depth - dims), :] = extra_rows(
            ones, half_norm(block.astype(jnp.float32)), depth - dims, width
        ).astype(jnp.bfloat16)

    def prepare_source(index, block):
        value = block.astype(jnp.float32)
        rows = [value, extra_rows(half_norm(value), ones, depth - dims, width)]
        sources[index] = jnp.concatenate(rows, axis=0).T.astype(jnp.bfloat16)

    def each_leaf(leaf, carry):
        prepare_target(leaf, points[leaf])
        prepare_source(local + leaf, points[leaf])
        prepare_source(leaf, near_points[0, leaf])
        prepare_source(2 * local + leaf, near_points[1, leaf])
        held_weights[leaf] = near_weights[0, leaf]
        held_weights[local + leaf] = weights[leaf]
        held_weights[2 * local + leaf] = near_weights[1, leaf]
        return carry

    lax.fori_loop(0, local, each_leaf, 0)

    def each_far(number, carry):
        prepare_target(local + number, far_points[number // local, number % local])
        return carry

    lax.fori_loop(0, (helpers - 1) * local, each_far, 0)

    total = tasks[2, 0]
    out[...] = jnp.zeros(out.shape, jnp.float32)

    def add_products(step):
        for part in range(TOGETHER):
            number = step * TOGETHER + part
            source, target = tasks[1, number], tasks[0, number]
            out[target] += jnp.dot(held_weights[source], kernels[part], preferred_element_type=jnp.float32)

    def take_exponentials():
        for part in range(TOGETHER):
            kernels[part] = jnp.exp(exponents[part]).astype(jnp.bfloat16)

    def find_exponents(step):
        for part in range(TOGETHER):
            number = step * TOGETHER + part
            source, target = tasks[1, number], tasks[0, number]
            exponents[part] = jnp.dot(sources[source], targets[target], preferred_element_type=jnp.float32)

    find_exponents(0)
    take_exponentials()
    find_exponents(1)

    def each_step(step, carry):
        add_products(step)
        take_exponentials()
        find_exponents(step + 2)
        return carry

    steps = lax.div(total + TOGETHER - 1, TOGETHER)
    lax.fori_loop(0, steps - 1, each_step, 0)

    @pl.when(total > 0)
    def _():
        add_products(steps - 1)

    own_sums[...] = out[pl.ds(0, local)]
    far_sums[...] = out[pl.ds(local, group - local)].astype(jnp.bfloat16).reshape(far_sums.shape)


def sum_pairs(helpers, points, weights, far_points, near_points, near_weights, tasks):
    local, dims, width = points.shape
    vectors = weights.shape[1]
    group = local * helpers
    vmem = pl.BlockSpec(memory_space=pltpu.VMEM)
    smem = pl.BlockSpec(memory_space=pltpu.SMEM)
    return pl.pallas_call(
        functools.partial(pairs_kernel, local, helpers),
        out_shape=(
            jax.ShapeDtypeStruct((local, vectors, width), jnp.float32),
            jax.ShapeDtypeStruct((helpers - 1, local, vectors, width), jnp.bfloat16),
        ),
        in_specs=[smem] + [vmem] * 5,
        out_specs=(vmem, vmem),
        scratch_shapes=[
            pltpu.VMEM((group + 1, vectors, width), jnp.float32),
            pltpu.VMEM((group + 1, dims + EXTRA, width), jnp.bfloat16),
            pltpu.VMEM((3 * local, width, dims + EXTRA), jnp.bfloat16),
            pltpu.VMEM((3 * local, vectors, width), jnp.bfloat16),
            pltpu.VMEM((TOGETHER, width, width), jnp.float32),
            pltpu.VMEM((TOGETHER, width, width), jnp.bfloat16),
        ],
        name="sum_pairs",
    )(tasks, points, weights, far_points, near_points, near_weights)


def return_kernel(helpers, far_sums, landed, send_sems, recv_sems):
    owner = lax.axis_index("owner")
    helper = lax.axis_index("helper")
    barrier = pltpu.get_barrier_semaphore()
    for distance in range(1, helpers):
        pl.semaphore_signal(
            barrier, inc=1, device_id=(owner, partner_of(helper, distance)), device_id_type=MESH
        )
    pl.semaphore_wait(barrier, helpers - 1)
    copies = []
    for distance in range(1, helpers):
        one = pltpu.make_async_remote_copy(
            src_ref=far_sums.at[distance - 1],
            dst_ref=landed.at[distance - 1],
            send_sem=send_sems.at[distance - 1],
            recv_sem=recv_sems.at[distance - 1],
            device_id=(owner, partner_of(helper, distance)),
            device_id_type=MESH,
        )
        one.start()
        copies.append(one)
    for one in copies:
        one.wait()


def return_sums(helpers, far_sums):
    any_space = pl.BlockSpec(memory_space=pl.ANY)
    return pl.pallas_call(
        functools.partial(return_kernel, helpers),
        out_shape=jax.ShapeDtypeStruct(far_sums.shape, far_sums.dtype),
        in_specs=[any_space],
        out_specs=any_space,
        scratch_shapes=[pltpu.SemaphoreType.DMA((helpers - 1,)), pltpu.SemaphoreType.DMA((helpers - 1,))],
        compiler_params=pltpu.CompilerParams(collective_id=1, has_side_effects=True),
        name="return_sums",
    )(far_sums)


def on_device(points, weights, neighbours, counts):
    owners = lax.axis_size("owner")
    helpers = lax.axis_size("helper")
    far_points, near_points, near_weights, tasks = gather_window(owners, helpers, points, weights, neighbours)
    own_sums, far_sums = sum_pairs(helpers, points, weights, far_points, near_points, near_weights, tasks)
    landed = return_sums(helpers, far_sums)
    return own_sums + jnp.sum(landed.astype(jnp.float32), axis=0)


def solution(mesh):
    placed = (
        P(("owner", "helper"), None, None),
        P(("owner", "helper"), None, None),
        P(("owner", "helper"), None),
        P(("owner", "helper")),
    )
    return jax.shard_map(
        on_device,
        mesh=mesh,
        in_specs=placed,
        out_specs=P(("owner", "helper"), None, None),
        check_vma=False,
    )
```

```python
import functools

import jax
import jax.numpy as jnp
from jax import lax
from jax.experimental import pallas as pl
from jax.experimental.pallas import tpu as pltpu
from jax.sharding import PartitionSpec as P

MESH = pl.DeviceIdType.MESH
EXTRA = 16
TOGETHER = 4


def partner_of(index, distance):
    result = index
    bit = 1
    while bit <= distance:
        if distance & bit:
            result = result + bit - 2 * bit * ((index // bit) % 2)
        bit *= 2
    return result


def list_tasks(base, helper, local, lists):
    group, slots = lists.shape
    count = 3 * local
    length = task_length(group, local)
    lists = jnp.where(lists < 0, -(1 << 20), lists)
    column = lax.broadcasted_iota(jnp.int32, (group, 128), 1)
    listed = []
    table = jnp.zeros((group, 128), jnp.float32)
    for source in range(count):
        leaf = base + (source // local) * group + helper * local + source % local
        one = jnp.max(jnp.where(lists == leaf, 1.0, 0.0), axis=1, keepdims=True)
        listed.append(one)
        table = jnp.where(column == source, one, table)
    below = lax.broadcasted_iota(jnp.int32, (group, group), 0) > lax.broadcasted_iota(jnp.int32, (group, group), 1)
    ahead = jnp.dot(
        jnp.where(below, 1.0, 0.0).astype(jnp.bfloat16), table.astype(jnp.bfloat16), preferred_element_type=jnp.float32
    )
    place = lax.broadcasted_iota(jnp.int32, (group, length), 1).astype(jnp.float32)
    row = lax.broadcasted_iota(jnp.int32, (group, length), 0).astype(jnp.float32)
    total = jnp.zeros((1, 1), jnp.float32)
    targets = jnp.zeros((group, length), jnp.float32)
    sources = jnp.zeros((group, length), jnp.float32)
    for source in range(count):
        here = jnp.where(listed[source] > 0.5, ahead[:, source:source + 1] + total, -1.0)
        targets = jnp.where(place == here, row, targets)
        sources = jnp.where(place == here, float(source), sources)
        total = total + jnp.sum(listed[source], axis=0, keepdims=True)
    target = jnp.where(place[:1] < total, jnp.sum(targets, axis=0, keepdims=True), float(group))
    source = jnp.sum(sources, axis=0, keepdims=True)
    line = lax.broadcasted_iota(jnp.int32, (8, length), 0)
    result = jnp.where(line == 0, target, jnp.where(line == 1, source, total))
    return result.astype(jnp.int32)


def task_length(group, local):
    return -(-(group * 3 * local + 3 * TOGETHER) // 128) * 128


def gather_kernel(owners, helpers, points, weights, lists, far_points, near_points, near_weights, tasks,
                  far_lists, send_sems, recv_sems):
    local = lists.shape[0]
    owner = lax.axis_index("owner")
    helper = lax.axis_index("helper")
    has_before = owner > 0
    has_after = owner < owners - 1
    barrier = pltpu.get_barrier_semaphore()
    for distance in range(1, helpers):
        pl.semaphore_signal(
            barrier, inc=1, device_id=(owner, partner_of(helper, distance)), device_id_type=MESH
        )

    @pl.when(has_before)
    def _():
        pl.semaphore_signal(barrier, inc=1, device_id=(owner - 1, helper), device_id_type=MESH)

    @pl.when(has_after)
    def _():
        pl.semaphore_signal(barrier, inc=1, device_id=(owner + 1, helper), device_id_type=MESH)

    neighbours = lax.min(owner, 1) + lax.min(owners - 1 - owner, 1)
    pl.semaphore_wait(barrier, helpers - 1 + neighbours)

    def copy(number, src, dst, device):
        return pltpu.make_async_remote_copy(
            src_ref=src,
            dst_ref=dst,
            send_sem=send_sems.at[number],
            recv_sem=recv_sems.at[number],
            device_id=device,
            device_id_type=MESH,
        )

    def beside(distance):
        return (owner, partner_of(helper, distance))

    number = 0
    list_copies = []
    for distance in range(1, helpers):
        list_copies.append(copy(number, lists, far_lists.at[distance - 1], beside(distance)))
        number += 1
    sent, relayed = [], []
    if helpers == 4 and local % 2 == 0:
        half = local // 2
        parts = (pl.ds(0, half), pl.ds(half, half))
        for order in (0, 1):
            for distance in (1, 2):
                part = parts[order if distance == 1 else 1 - order]
                one = copy(number, points.at[part], far_points.at[distance - 1, part], beside(distance))
                number += 1
                sent.append(one)
        for distance in (1, 2):
            part = parts[distance - 1]
            block = far_points.at[distance - 1, part]
            one = copy(number, block, far_points.at[2, part], beside(3 - distance))
            number += 1
            relayed.append(one)
    else:
        for distance in range(1, helpers):
            sent.append(copy(number, points, far_points.at[distance - 1], beside(distance)))
            number += 1
    up = [
        copy(number, points, near_points.at[0], (owner + 1, helper)),
        copy(number + 1, weights, near_weights.at[0], (owner + 1, helper)),
    ]
    down = [
        copy(number + 2, points, near_points.at[1], (owner - 1, helper)),
        copy(number + 3, weights, near_weights.at[1], (owner - 1, helper)),
    ]
    for one in list_copies + sent:
        one.start()

    @pl.when(has_after)
    def _():
        for one in up:
            one.start()

    @pl.when(has_before)
    def _():
        for one in down:
            one.start()

    for place, one in enumerate(relayed):
        sent[place].wait_recv()
        one.start()
    for one in list_copies:
        one.wait_recv()
    whole = jnp.concatenate([lists[...]] + [far_lists[i] for i in range(helpers - 1)], axis=0)
    tasks[...] = list_tasks((owner - 1) * local * helpers, helper, local, whole)
    for one in sent[len(relayed):] + relayed:
        one.wait_recv()
    for one in list_copies + sent + relayed:
        one.wait_send()

    @pl.when(has_after)
    def _():
        for one in up:
            one.wait_send()
        for one in down:
            one.wait_recv()

    @pl.when(has_before)
    def _():
        for one in down:
            one.wait_send()
        for one in up:
            one.wait_recv()


def gather_window(owners, helpers, points, weights, lists):
    local = points.shape[0]
    copies = 2 * (helpers - 1) + 10
    vmem = pl.BlockSpec(memory_space=pltpu.VMEM)
    any_space = pl.BlockSpec(memory_space=pl.ANY)
    return pl.pallas_call(
        functools.partial(gather_kernel, owners, helpers),
        out_shape=(
            jax.ShapeDtypeStruct((helpers - 1,) + points.shape, points.dtype),
            jax.ShapeDtypeStruct((2,) + points.shape, points.dtype),
            jax.ShapeDtypeStruct((2,) + weights.shape, weights.dtype),
            jax.ShapeDtypeStruct((8, task_length(local * helpers, local)), jnp.int32),
        ),
        in_specs=[any_space, any_space, vmem],
        out_specs=(any_space, any_space, any_space, vmem),
        scratch_shapes=[
            pltpu.VMEM((helpers - 1,) + lists.shape, lists.dtype),
            pltpu.SemaphoreType.DMA((copies,)),
            pltpu.SemaphoreType.DMA((copies,)),
        ],
        compiler_params=pltpu.CompilerParams(collective_id=0, has_side_effects=True),
        name="gather_window",
    )(points, weights, lists)


def pieces_of(value, count):
    parts = []
    for _ in range(count):
        part = value.astype(jnp.bfloat16).astype(jnp.float32)
        parts.append(part)
        value = value - part
    return parts


def extra_rows(first, second, rows, width):
    row = lax.broadcasted_iota(jnp.int32, (rows, width), 0)
    result = jnp.zeros((rows, width), jnp.float32)
    for i, value in enumerate(list(first) + list(second)):
        result = jnp.where(row == i, value, result)
    return result


def pairs_kernel(local, helpers, tasks, points, weights, far_points, near_points, near_weights,
                 own_sums, far_sums, out, targets, sources, held_weights, exponents, kernels):
    dims, width = points.shape[1:]
    group = local * helpers
    depth = targets.shape[1]
    ones = [jnp.ones((1, width), jnp.float32)] * 3

    def half_norm(value):
        return pieces_of(-0.5 * jnp.sum(value * value, axis=0, keepdims=True), 3)

    def prepare_target(index, block):
        targets[index, pl.ds(0, dims), :] = block
        targets[index, pl.ds(dims, depth - dims), :] = extra_rows(
            ones, half_norm(block.astype(jnp.float32)), depth - dims, width
        ).astype(jnp.bfloat16)

    def prepare_source(index, block):
        value = block.astype(jnp.float32)
        rows = [value, extra_rows(half_norm(value), ones, depth - dims, width)]
        sources[index] = jnp.concatenate(rows, axis=0).T.astype(jnp.bfloat16)

    def each_leaf(leaf, carry):
        prepare_target(leaf, points[leaf])
        prepare_source(local + leaf, points[leaf])
        prepare_source(leaf, near_points[0, leaf])
        prepare_source(2 * local + leaf, near_points[1, leaf])
        held_weights[leaf] = near_weights[0, leaf]
        held_weights[local + leaf] = weights[leaf]
        held_weights[2 * local + leaf] = near_weights[1, leaf]
        return carry

    for leaf in range(local):
        each_leaf(leaf, 0)

    def each_far(distance, carry):
        for leaf in range(local):
            prepare_target((distance + 1) * local + leaf, far_points[distance, leaf])
        return carry

    lax.fori_loop(0, helpers - 1, each_far, 0)

    total = tasks[2, 0]
    out[...] = jnp.zeros(out.shape, jnp.float32)

    def add_products(step):
        for part in range(TOGETHER):
            number = step * TOGETHER + part
            source, target = tasks[1, number], tasks[0, number]
            out[target] += jnp.dot(held_weights[source], kernels[part], preferred_element_type=jnp.float32)

    def take_exponentials():
        for part in range(TOGETHER):
            kernels[part] = jnp.exp(exponents[part]).astype(jnp.bfloat16)

    def find_exponents(step):
        for part in range(TOGETHER):
            number = step * TOGETHER + part
            source, target = tasks[1, number], tasks[0, number]
            exponents[part] = jnp.dot(sources[source], targets[target], preferred_element_type=jnp.float32)

    find_exponents(0)
    take_exponentials()
    find_exponents(1)

    def each_step(step, carry):
        add_products(step)
        take_exponentials()
        find_exponents(step + 2)
        return carry

    steps = lax.div(total + TOGETHER - 1, TOGETHER)
    lax.fori_loop(0, steps - 1, each_step, 0)

    @pl.when(total > 0)
    def _():
        add_products(steps - 1)

    own_sums[...] = out[pl.ds(0, local)]
    far_sums[...] = out[pl.ds(local, group - local)].astype(jnp.bfloat16).reshape(far_sums.shape)


def sum_pairs(helpers, points, weights, far_points, near_points, near_weights, tasks):
    local, dims, width = points.shape
    vectors = weights.shape[1]
    group = local * helpers
    vmem = pl.BlockSpec(memory_space=pltpu.VMEM)
    smem = pl.BlockSpec(memory_space=pltpu.SMEM)
    return pl.pallas_call(
        functools.partial(pairs_kernel, local, helpers),
        out_shape=(
            jax.ShapeDtypeStruct((local, vectors, width), jnp.float32),
            jax.ShapeDtypeStruct((helpers - 1, local, vectors, width), jnp.bfloat16),
        ),
        in_specs=[smem] + [vmem] * 5,
        out_specs=(vmem, vmem),
        scratch_shapes=[
            pltpu.VMEM((group + 1, vectors, width), jnp.float32),
            pltpu.VMEM((group + 1, dims + EXTRA, width), jnp.bfloat16),
            pltpu.VMEM((3 * local, width, dims + EXTRA), jnp.bfloat16),
            pltpu.VMEM((3 * local, vectors, width), jnp.bfloat16),
            pltpu.VMEM((TOGETHER, width, width), jnp.float32),
            pltpu.VMEM((TOGETHER, width, width), jnp.bfloat16),
        ],
        name="sum_pairs",
    )(tasks, points, weights, far_points, near_points, near_weights)


def return_kernel(helpers, far_sums, landed, send_sems, recv_sems):
    owner = lax.axis_index("owner")
    helper = lax.axis_index("helper")
    barrier = pltpu.get_barrier_semaphore()
    for distance in range(1, helpers):
        pl.semaphore_signal(
            barrier, inc=1, device_id=(owner, partner_of(helper, distance)), device_id_type=MESH
        )
    pl.semaphore_wait(barrier, helpers - 1)
    copies = []
    for distance in range(1, helpers):
        one = pltpu.make_async_remote_copy(
            src_ref=far_sums.at[distance - 1],
            dst_ref=landed.at[distance - 1],
            send_sem=send_sems.at[distance - 1],
            recv_sem=recv_sems.at[distance - 1],
            device_id=(owner, partner_of(helper, distance)),
            device_id_type=MESH,
        )
        one.start()
        copies.append(one)
    for one in copies:
        one.wait()


def return_sums(helpers, far_sums):
    any_space = pl.BlockSpec(memory_space=pl.ANY)
    return pl.pallas_call(
        functools.partial(return_kernel, helpers),
        out_shape=jax.ShapeDtypeStruct(far_sums.shape, far_sums.dtype),
        in_specs=[any_space],
        out_specs=any_space,
        scratch_shapes=[pltpu.SemaphoreType.DMA((helpers - 1,)), pltpu.SemaphoreType.DMA((helpers - 1,))],
        compiler_params=pltpu.CompilerParams(collective_id=1, has_side_effects=True),
        name="return_sums",
    )(far_sums)


def on_device(points, weights, neighbours, counts):
    owners = lax.axis_size("owner")
    helpers = lax.axis_size("helper")
    far_points, near_points, near_weights, tasks = gather_window(owners, helpers, points, weights, neighbours)
    own_sums, far_sums = sum_pairs(helpers, points, weights, far_points, near_points, near_weights, tasks)
    landed = return_sums(helpers, far_sums)
    return own_sums + jnp.sum(landed.astype(jnp.float32), axis=0)


def solution(mesh):
    placed = (
        P(("owner", "helper"), None, None),
        P(("owner", "helper"), None, None),
        P(("owner", "helper"), None),
        P(("owner", "helper")),
    )
    return jax.shard_map(
        on_device,
        mesh=mesh,
        in_specs=placed,
        out_specs=P(("owner", "helper"), None, None),
        check_vma=False,
    )
```
